32 devices in a mesh: dp: 4 (over y, core), shard: 8 (over z, x).
Axes of the slice: x: 2, y: 2, z: 4, core: 2. Of those that a mesh axis runs over, the one named last changes fastest.
Arguments:
- inputs: bfloat16 [2, 32, 512, 768], P(None, ('dp', 'shard')), may hold values from -6 to 6
- doc_ids: int32 [2, 32, 512], P(None, ('dp', 'shard')), may hold values from -1 to 7, as said below
- first_gain: bfloat16 [768], P(('dp', 'shard')), may hold values from 0.5 to 1.5
- first_shift: bfloat16 [768], P(('dp', 'shard')), may hold values from -1.5 to 1.5
- query_weight: bfloat16 [768, 768], P(('dp', 'shard')), may hold values from -0.21875 to 0.21875
- query_bias: bfloat16 [768], P(('dp', 'shard')), may hold values from -1.5 to 1.5
- key_weight: bfloat16 [768, 768], P(('dp', 'shard')), may hold values from -0.21875 to 0.21875
- value_weight: bfloat16 [768, 768], P(('dp', 'shard')), may hold values from -0.21875 to 0.21875
- value_bias: bfloat16 [768], P(('dp', 'shard')), may hold values from -1.5 to 1.5
- second_gain: bfloat16 [768], P(('dp', 'shard')), may hold values from 0.5 to 1.5
- second_shift: bfloat16 [768], P(('dp', 'shard')), may hold values from -1.5 to 1.5
- output_weight: bfloat16 [768, 768], P(('dp', 'shard')), may hold values from -0.21875 to 0.21875
- output_bias: bfloat16 [768], P(('dp', 'shard')), may hold values from -1.5 to 1.5
- third_gain: bfloat16 [768], P(('dp', 'shard')), may hold values from 0.5 to 1.5
- third_shift: bfloat16 [768], P(('dp', 'shard')), may hold values from -1.5 to 1.5
- up_weight: bfloat16 [768, 3072], P(('dp', 'shard')), may hold values from -0.21875 to 0.21875
- up_bias: bfloat16 [3072], P(('dp', 'shard')), may hold values from -1.5 to 1.5
- fourth_gain: bfloat16 [3072], P(('dp', 'shard')), may hold values from 0.5 to 1.5
- fourth_shift: bfloat16 [3072], P(('dp', 'shard')), may hold values from -1.5 to 1.5
- down_weight: bfloat16 [3072, 768], P(('dp', 'shard')), may hold values from -0.109375 to 0.109375
- down_bias: bfloat16 [768], P(('dp', 'shard')), may hold values from -1.5 to 1.5
- cotangent: bfloat16 [2, 32, 512, 768], P(None, ('dp', 'shard')), may hold values from -6 to 6
Outputs:
- layer_out: bfloat16 [2, 32, 512, 768], P(None, ('dp', 'shard'))
- input_grad: bfloat16 [2, 32, 512, 768], P(None, ('dp', 'shard'))
- first_gain_grad: float32 [768], P(('dp', 'shard'))
- first_shift_grad: float32 [768], P(('dp', 'shard'))
- query_weight_grad: float32 [768, 768], P(('dp', 'shard'))
- query_bias_grad: float32 [768], P(('dp', 'shard'))
- key_weight_grad: float32 [768, 768], P(('dp', 'shard'))
- value_weight_grad: float32 [768, 768], P(('dp', 'shard'))
- value_bias_grad: float32 [768], P(('dp', 'shard'))
- second_gain_grad: float32 [768], P(('dp', 'shard'))
- second_shift_grad: float32 [768], P(('dp', 'shard'))
- output_weight_grad: float32 [768, 768], P(('dp', 'shard'))
- output_bias_grad: float32 [768], P(('dp', 'shard'))
- third_gain_grad: float32 [768], P(('dp', 'shard'))
- third_shift_grad: float32 [768], P(('dp', 'shard'))
- up_weight_grad: float32 [768, 3072], P(('dp', 'shard'))
- up_bias_grad: float32 [3072], P(('dp', 'shard'))
- fourth_gain_grad: float32 [3072], P(('dp', 'shard'))
- fourth_shift_grad: float32 [3072], P(('dp', 'shard'))
- down_weight_grad: float32 [3072, 768], P(('dp', 'shard'))
- down_bias_grad: float32 [768], P(('dp', 'shard'))
The draws below stay inside these ranges and needn't reach their ends.
Inputs may be any that keep to these rules, and one draw needn't show every extreme that they name: `doc_ids`: in each row the ids start at 0 and rise by one from document to document; documents hold 64, 128, 256 or 512 tokens, the last one cut by the row's end; then 1 to 64 padding tokens of id -1 overwrite the row's tail; one row of every draw holds eight documents of 64 tokens, the eighth shortened by its padding.
All inputs are finite; a program needn't handle non-finite values.
Results may differ from the reference program's by a relative error of at most 0.014.
Values may be sent and summed in bfloat16 or wider, within the bound.
A program may use at most 320 MiB of HBM per device.

```python
import math
import jax
import jax.numpy as jnp
from jax import lax

D = 768
HD = 64
FF = 3072
ROW = 512
MICRO = 2
ROWS = 32


def draw_doc_ids(key, part):
    total_rows = MICRO * ROWS
    length_key, padding_key, chosen_key = jax.random.split(key, 3)
    levels = jax.random.randint(length_key, (total_rows, 8), 0, 16)
    chosen = jax.random.randint(chosen_key, (), 0, total_rows)
    row_index = jnp.arange(total_rows, dtype=jnp.int32)
    levels = jnp.where(row_index[:, None] == chosen, 15, levels)
    shifts = 3 - (levels >= 1).astype(jnp.int32) - (levels >= 3).astype(jnp.int32) - (levels >= 7).astype(jnp.int32)
    lengths = ROW // 8 * jnp.left_shift(jnp.ones_like(shifts), shifts)
    ends = jnp.cumsum(lengths, axis=1)
    padding = jax.random.randint(padding_key, (total_rows, 1), 1, ROW // 8 + 1)
    padding = jnp.where(row_index[:, None] == chosen, jnp.minimum(padding, ROW // 8 - 1), padding)
    places = jnp.arange(ROW, dtype=jnp.int32)
    docs = jnp.sum((places[None, :, None] >= ends[:, None, :]).astype(jnp.int32), axis=2)
    docs = jnp.where(places[None, :] < ROW - padding, docs, -1)
    return docs.reshape(MICRO, ROWS, ROW).astype(jnp.int32)


def block_scale(rng, dims, cuts, least, top_value):
    loudness = 1.0
    for position, parts in cuts:
        heights = jax.random.uniform(jax.random.fold_in(jax.random.fold_in(rng, 6), position), (parts,), jnp.float32, least / len(cuts), top_value / len(cuts))
        loudness = loudness * jnp.repeat(jnp.exp(heights), dims[position] // parts).reshape((-1,) + (1,) * (len(dims) - 1 - position))
    return loudness


def centred(rng, shape, scale, reach, pieces=(), kind=jnp.bfloat16):
    level = block_scale(rng, shape, pieces, -0.22, 0.18) if pieces else 1.0
    values = jax.random.normal(rng, shape, jnp.float32) * scale * level
    return jnp.minimum(jnp.maximum(values, -reach), reach).astype(kind)


def setup_inputs(seed: int = 0) -> dict:
    key_of = jax.random.split(jax.random.key(seed), 23)
    inputs = centred(key_of[0], (MICRO, ROWS, ROW, D), 1.0, 6.0, ((1, 32),))
    doc_ids = draw_doc_ids(jax.random.fold_in(key_of[22], 71), 0)
    first_gain = jnp.clip(1.0 + 0.1 * jax.random.normal(key_of[2], (D,), jnp.float32), 0.5, 1.5).astype(jnp.bfloat16)
    first_shift = centred(key_of[3], (D,), 0.3, 1.5, ((0, 32),))
    query_weight = centred(key_of[4], (D, D), D ** -0.5, 0.21875, ((0, 32),))
    query_bias = centred(key_of[5], (D,), 0.3, 1.5, ((0, 32),))
    key_weight = centred(key_of[6], (D, D), D ** -0.5, 0.21875, ((0, 32),))
    value_weight = centred(key_of[7], (D, D), D ** -0.5, 0.21875, ((0, 32),))
    value_bias = centred(key_of[8], (D,), 0.3, 1.5, ((0, 32),))
    second_gain = jnp.clip(1.0 + 0.1 * jax.random.normal(key_of[9], (D,), jnp.float32), 0.5, 1.5).astype(jnp.bfloat16)
    second_shift = centred(key_of[10], (D,), 0.3, 1.5, ((0, 32),))
    output_weight = centred(key_of[11], (D, D), D ** -0.5, 0.21875, ((0, 32),))
    output_bias = centred(key_of[12], (D,), 0.3, 1.5, ((0, 32),))
    third_gain = jnp.clip(1.0 + 0.1 * jax.random.normal(key_of[13], (D,), jnp.float32), 0.5, 1.5).astype(jnp.bfloat16)
    third_shift = centred(key_of[14], (D,), 0.3, 1.5, ((0, 32),))
    up_weight = centred(key_of[15], (D, FF), D ** -0.5, 0.21875, ((0, 32),))
    up_bias = centred(key_of[16], (FF,), 0.3, 1.5, ((0, 32),))
    fourth_gain = jnp.clip(1.0 + 0.1 * jax.random.normal(key_of[17], (FF,), jnp.float32), 0.5, 1.5).astype(jnp.bfloat16)
    fourth_shift = centred(key_of[18], (FF,), 0.3, 1.5, ((0, 32),))
    down_weight = centred(key_of[19], (FF, D), FF ** -0.5, 0.109375, ((0, 32),))
    down_bias = centred(key_of[20], (D,), 0.3, 1.5, ((0, 32),))
    cotangent = centred(key_of[21], (MICRO, ROWS, ROW, D), 1.0, 6.0, ((1, 32),))
    return {"inputs": inputs, "doc_ids": doc_ids, "first_gain": first_gain, "first_shift": first_shift, "query_weight": query_weight, "query_bias": query_bias, "key_weight": key_weight, "value_weight": value_weight, "value_bias": value_bias, "second_gain": second_gain, "second_shift": second_shift, "output_weight": output_weight, "output_bias": output_bias, "third_gain": third_gain, "third_shift": third_shift, "up_weight": up_weight, "up_bias": up_bias, "fourth_gain": fourth_gain, "fourth_shift": fourth_shift, "down_weight": down_weight, "down_bias": down_bias, "cotangent": cotangent}


@jax.custom_vjp
def low(v):
    return lax.optimization_barrier(v.astype(jnp.bfloat16)).astype(jnp.float32)

@jax.custom_vjp
def low_back(v):
    return v

def low_keep(v):
    return (low(v), None)

def low_pass(kept, grad):
    return (grad,)

def back_keep(v):
    return (v, None)

def back_low(kept, grad):
    return (low(grad),)
low.defvjp(low_keep, low_pass)
low_back.defvjp(back_keep, back_low)

def matmul_high(left, right):
    return jnp.matmul(left, right, precision=lax.Precision.HIGHEST)

def layer_norm(values, gain, shift):
    center = values - lax.optimization_barrier(jnp.mean(values, axis=-1, keepdims=True))
    inverse = lax.rsqrt(lax.optimization_barrier(jnp.mean(center * center, axis=-1, keepdims=True)) + 1e-05)
    return center * inverse * gain + shift

def layer(params, tokens, ids):
    first_gain, first_shift, query_weight, query_bias, key_weight, value_weight, value_bias, second_gain, second_shift, output_weight, output_bias, third_gain, third_shift, up_weight, up_bias, fourth_gain, fourth_shift, down_weight, down_bias = params
    groups, length, width = tokens.shape
    normed = low(layer_norm(tokens, first_gain, first_shift))
    query = low(low_back(matmul_high(normed, query_weight) + query_bias))
    keys = low(low_back(matmul_high(normed, key_weight)))
    values = low(low_back(matmul_high(normed, value_weight) + value_bias))
    query = query.reshape(groups, length, width // HD, HD)
    keys = keys.reshape(groups, length, width // HD, HD)
    values = values.reshape(groups, length, width // HD, HD)
    scores = jnp.einsum('gqhd,gkhd->ghqk', query, keys, precision=lax.Precision.HIGHEST) * HD ** (-0.5)
    scores = low_back(scores)
    places = lax.broadcasted_iota(jnp.int32, (length, length), 0)
    others = lax.broadcasted_iota(jnp.int32, (length, length), 1)
    allowed = (ids[:, :, None] == ids[:, None, :]) & (ids[:, None, :] >= 0) | (places == others)[None]
    scores = jnp.where(allowed[:, None], scores, -1e+30)
    probs = low(jax.nn.softmax(scores, axis=-1))
    mixed = jnp.einsum('ghqk,gkhd->gqhd', probs, values, precision=lax.Precision.HIGHEST)
    mixed = low_back(mixed.reshape(groups, length, width))
    branch = low(layer_norm(mixed, second_gain, second_shift))
    residual = tokens + low_back(matmul_high(branch, output_weight) + output_bias)
    feed_in = low(layer_norm(residual, third_gain, third_shift))
    upper = low_back(matmul_high(feed_in, up_weight) + up_bias)
    down_in = low(layer_norm(jax.nn.gelu(upper, approximate=False), fourth_gain, fourth_shift))
    return residual + low_back(matmul_high(down_in, down_weight) + down_bias)

def reference(inputs, doc_ids, first_gain, first_shift, query_weight, query_bias, key_weight, value_weight, value_bias, second_gain, second_shift, output_weight, output_bias, third_gain, third_shift, up_weight, up_bias, fourth_gain, fourth_shift, down_weight, down_bias, cotangent):
    params = tuple((piece.astype(jnp.float32) for piece in (first_gain, first_shift, query_weight, query_bias, key_weight, value_weight, value_bias, second_gain, second_shift, output_weight, output_bias, third_gain, third_shift, up_weight, up_bias, fourth_gain, fourth_shift, down_weight, down_bias)))
    length = inputs.shape[2]
    width = inputs.shape[3]
    total_rows = inputs.shape[0] * inputs.shape[1]
    group = math.gcd(total_rows, max(1, 4096 // length))
    count = total_rows // group
    tokens = inputs.astype(jnp.float32).reshape(count, group, length, width)
    ids = doc_ids.reshape(count, group, length).astype(jnp.int32)
    incoming = cotangent.astype(jnp.float32).reshape(count, group, length, width)

    def step(carry, block):
        token_block, id_block, grad_block = block
        result, pullback = jax.vjp(lambda weights, values: layer(weights, values, id_block), params, token_block)
        weight_grads, token_grad = pullback(grad_block)
        return (jax.tree.map(jnp.add, carry, weight_grads), (result, token_grad))
    zeros = tuple((jnp.zeros_like(piece) for piece in params))
    sums, (results, token_grads) = lax.scan(step, zeros, (tokens, ids, incoming))
    first_gain_grad, first_shift_grad, query_weight_grad, query_bias_grad, key_weight_grad, value_weight_grad, value_bias_grad, second_gain_grad, second_shift_grad, output_weight_grad, output_bias_grad, third_gain_grad, third_shift_grad, up_weight_grad, up_bias_grad, fourth_gain_grad, fourth_shift_grad, down_weight_grad, down_bias_grad = sums
    layer_out = results.reshape(inputs.shape).astype(jnp.bfloat16)
    input_grad = token_grads.reshape(inputs.shape).astype(jnp.bfloat16)
    return (layer_out, input_grad, first_gain_grad, first_shift_grad, query_weight_grad, query_bias_grad, key_weight_grad, value_weight_grad, value_bias_grad, second_gain_grad, second_shift_grad, output_weight_grad, output_bias_grad, third_gain_grad, third_shift_grad, up_weight_grad, up_bias_grad, fourth_gain_grad, fourth_shift_grad, down_weight_grad, down_bias_grad)
```

```python
import functools

import jax
import jax.numpy as jnp
from jax import lax
from jax.experimental import pallas as pl
from jax.experimental.pallas import tpu as pltpu
from jax.sharding import PartitionSpec as P


MESH = pl.DeviceIdType.MESH
AXES = ("dp", "shard")


class Grid:
    def __init__(self, dp, shard):
        self.ny = dp // 2
        self.nx = self.ny
        self.nz = shard // self.nx

    def here(self):
        dp, shard = lax.axis_index("dp"), lax.axis_index("shard")
        return dp // 2, dp % 2, shard // self.nx, shard % self.nx

    def device(self, y, c, z, x):
        return (y * 2 + c, z * self.nx + x)

    def blocks(self):
        return (self.ny, 2, self.nz, self.nx)


def others(size, mine):
    return [lax.rem(mine + k, size) for k in range(1, size)]


def greet(grid, y, c, z, x):
    barrier = pltpu.get_barrier_semaphore()
    peers = (
        [(y, c, p, x) for p in others(grid.nz, z)]
        + [(y, c, z, p) for p in others(grid.nx, x)]
        + [(p, c, z, x) for p in others(grid.ny, y)]
        + [(y, 1 - c, z, x)]
    )
    for peer in peers:
        pl.semaphore_signal(barrier, inc=1, device_id=grid.device(*peer), device_id_type=MESH)
    pl.semaphore_wait(barrier, len(peers))


class Gather:
    def __init__(self, grid, place, source, target, colour, send, recv, local):
        self.g, self.place = grid, place
        self.source, self.target, self.colour = source, target, colour
        self.send, self.recv, self.local = send, recv, local

    def plan(self, phase):
        g = self.g
        y, c, z, x = self.place
        t = self.target
        if phase == 0:
            return [(self.source, t.at[y, c, z, x], t.at[y, c, p, x], (y, c, p, x), z, p) for p in others(g.nz, z)]
        if phase == 3:
            return [(t.at[:, c], t.at[:, c], t.at[:, 1 - c], (y, 1 - c, z, x), c, 1 - c)]
        along_x = (phase == 1) == (self.colour == 0)
        if along_x:
            cut = (lambda p: t.at[y, c, :, p]) if phase == 1 else (lambda p: t.at[:, c, :, p])
            return [(cut(x), cut(x), cut(p), (y, c, z, p), x, p) for p in others(g.nx, x)]
        cut = (lambda p: t.at[p, c, :, x]) if phase == 1 else (lambda p: t.at[p, c])
        return [(cut(y), cut(y), cut(p), (p, c, z, x), y, p) for p in others(g.ny, y)]

    def go(self, phase, entry):
        src, dst, _, peer, mine, theirs = entry
        return pltpu.make_async_remote_copy(
            src_ref=src, dst_ref=dst, send_sem=self.send.at[phase, theirs], recv_sem=self.recv.at[phase, mine],
            device_id=self.g.device(*peer), device_id_type=MESH)

    def come(self, phase, entry):
        _, _, landed, peer, _, theirs = entry
        return pltpu.make_async_remote_copy(
            src_ref=landed, dst_ref=landed, send_sem=self.send.at[phase, theirs], recv_sem=self.recv.at[phase, theirs],
            device_id=self.g.device(*peer), device_id_type=MESH)

    def own(self):
        y, c, z, x = self.place
        return pltpu.make_async_copy(self.source, self.target.at[y, c, z, x], self.local)

    def start(self, phase):
        if phase == 0:
            self.own().start()
        for entry in self.plan(phase):
            self.go(phase, entry).start()

    def arrive(self, phase):
        if phase == 0:
            self.own().wait()
        for entry in self.plan(phase):
            self.come(phase, entry).wait_recv()

    def drain(self):
        for phase in range(4):
            for entry in self.plan(phase):
                self.go(phase, entry).wait_send()


def gather_kernel(grid, colours, *refs):
    n = len(colours)
    sources, targets, (send, recv, local) = refs[:n], refs[n : 2 * n], refs[2 * n :]
    place = grid.here()
    greet(grid, *place)
    jobs = [
        Gather(grid, place, sources[i], targets[i], colours[i], send.at[i], recv.at[i], local.at[i]) for i in range(n)
    ]
    for job in jobs:
        job.start(0)
    for tick in range(n + 2):
        for phase in (3, 2, 1):
            i = tick - (phase - 1)
            if 0 <= i < n:
                jobs[i].arrive(phase - 1)
                jobs[i].start(phase)
    for job in jobs:
        job.arrive(3)
    for job in jobs:
        job.drain()


def gather_all(grid, pieces, colours, collective_id):
    n = len(pieces)
    wide = max(grid.nx, grid.ny, grid.nz, 2)
    outs = pl.pallas_call(
        functools.partial(gather_kernel, grid, colours),
        out_shape=[jax.ShapeDtypeStruct(grid.blocks() + p.shape, p.dtype) for p in pieces],
        in_specs=[pl.BlockSpec(memory_space=pltpu.VMEM)] * n,
        out_specs=[pl.BlockSpec(memory_space=pl.ANY)] * n,
        scratch_shapes=[
            pltpu.SemaphoreType.DMA((n, 4, wide)),
            pltpu.SemaphoreType.DMA((n, 4, wide)),
            pltpu.SemaphoreType.DMA((n,)),
        ],
        compiler_params=pltpu.CompilerParams(collective_id=collective_id, has_side_effects=True),
        name="gather_parameters",
    )(*pieces)
    return outs


class Scatter:
    def __init__(self, grid, place, source, target, held, land, colour, send, recv, local):
        self.g, self.place, self.colour = grid, place, colour
        self.source, self.target, self.held, self.land = source, target, held, land
        self.send, self.recv, self.local = send, recv, local

    def along_y(self, phase):
        return (phase == 1) == (self.colour == 0)

    def plan(self, phase):
        g, held, land = self.g, self.held, self.land
        y, c, z, x = self.place
        if phase == 0:
            return [(self.source.at[:, 1 - c], lambda s: land[0], (y, 1 - c, z, x), c, 1 - c)]
        if phase == 3:
            return [(held.at[y, p, x], lambda s: land[3].at[s], (y, c, p, x), z, p) for p in others(g.nz, z)]
        if self.along_y(phase):
            cut = (lambda p: held.at[p]) if phase == 1 else (lambda p: held.at[p, :, x])
            return [(cut(p), lambda s: land[phase].at[s], (p, c, z, x), y, p) for p in others(g.ny, y)]
        cut = (lambda p: held.at[:, :, p]) if phase == 1 else (lambda p: held.at[y, :, p])
        return [(cut(p), lambda s: land[phase].at[s], (y, c, z, p), x, p) for p in others(g.nx, x)]

    def own(self):
        return pltpu.make_async_copy(self.source.at[:, self.place[1]], self.held, self.local)

    def go(self, phase, entry):
        src, spot, peer, mine, theirs = entry
        return pltpu.make_async_remote_copy(
            src_ref=src, dst_ref=spot(mine), send_sem=self.send.at[phase, theirs], recv_sem=self.recv.at[phase, mine],
            device_id=self.g.device(*peer), device_id_type=MESH)

    def come(self, phase, entry):
        src, spot, peer, mine, theirs = entry
        return pltpu.make_async_remote_copy(
            src_ref=spot(theirs), dst_ref=spot(theirs), send_sem=self.send.at[phase, theirs],
            recv_sem=self.recv.at[phase, theirs], device_id=self.g.device(*peer), device_id_type=MESH)

    def start(self, phase):
        if phase == 0:
            self.own().start()
        for entry in self.plan(phase):
            self.go(phase, entry).start()

    def finish(self, phase):
        g, held, land = self.g, self.held, self.land
        y, c, z, x = self.place
        if phase == 0:
            self.own().wait()
        plan = self.plan(phase)
        for entry in plan:
            self.come(phase, entry).wait_recv()
        kind = held.dtype
        f32 = jnp.float32

        def add(at, parts, out=None):
            total = held[at].astype(f32)
            for part in parts:
                total = total + part.astype(f32)
            if out is None:
                held[at] = total.astype(kind)
            else:
                out[...] = total

        slots = [entry[4] for entry in plan]
        if phase == 0:
            def body(i, carry):
                at = (i // (g.nz * g.nx), i // g.nx % g.nz, i % g.nx)
                add(at, [land[0][at]])
                return carry
            lax.fori_loop(0, g.ny * g.nz * g.nx, body, 0)
        elif phase == 3:
            add((y, z, x), [land[3][s] for s in slots], self.target)
        elif phase == 1 and self.along_y(1):
            def body(i, carry):
                add((y, i // g.nx, i % g.nx), [land[1][s, i // g.nx, i % g.nx] for s in slots])
                return carry
            lax.fori_loop(0, g.nz * g.nx, body, 0)
        elif phase == 1:
            def body(i, carry):
                add((i // g.nz, i % g.nz, x), [land[1][s, i // g.nz, i % g.nz] for s in slots])
                return carry
            lax.fori_loop(0, g.ny * g.nz, body, 0)
        else:
            def body(i, carry):
                add((y, i, x), [land[2][s, i] for s in slots])
                return carry
            lax.fori_loop(0, g.nz, body, 0)

    def drain(self):
        for phase in range(4):
            for entry in self.plan(phase):
                self.go(phase, entry).wait_send()


def scatter_scratch(grid, piece, kind, colour):
    ny, nz, nx = grid.ny, grid.nz, grid.nx
    if colour == 0:
        one, two = (ny, nz, nx), (nx, nz)
    else:
        one, two = (nx, ny, nz), (ny, nz)
    return [pltpu.VMEM(s + piece, kind) for s in ((ny, nz, nx), (ny, nz, nx), one, two, (nz,))]


def scatter_kernel(grid, colours, *refs):
    n = len(colours)
    sources, targets = refs[:n], refs[n : 2 * n]
    bufs = refs[2 * n : 7 * n]
    send, recv, local = refs[7 * n :]
    place = grid.here()
    greet(grid, *place)
    jobs = [
        Scatter(grid, place, sources[i], targets[i], bufs[5 * i], bufs[5 * i + 1 : 5 * i + 5], colours[i],
                send.at[i], recv.at[i], local.at[i])
        for i in range(n)
    ]
    for job in jobs:
        job.start(0)
    for tick in range(n + 2):
        for phase in (3, 2, 1):
            i = tick - (phase - 1)
            if 0 <= i < n:
                jobs[i].finish(phase - 1)
                jobs[i].start(phase)
    for job in jobs:
        job.finish(3)
    for job in jobs:
        job.drain()


def scatter_all(grid, arrays, colours, collective_id):
    n = len(arrays)
    wide = max(grid.nx, grid.ny, grid.nz, 2)
    scratch = []
    for a, colour in zip(arrays, colours):
        scratch += scatter_scratch(grid, a.shape[4:], a.dtype, colour)
    return pl.pallas_call(
        functools.partial(scatter_kernel, grid, colours),
        out_shape=[jax.ShapeDtypeStruct(a.shape[4:], jnp.float32) for a in arrays],
        in_specs=[pl.BlockSpec(memory_space=pl.ANY)] * n,
        out_specs=[pl.BlockSpec(memory_space=pltpu.VMEM)] * n,
        scratch_shapes=scratch + [
            pltpu.SemaphoreType.DMA((n, 4, wide)),
            pltpu.SemaphoreType.DMA((n, 4, wide)),
            pltpu.SemaphoreType.DMA((n,)),
        ],
        compiler_params=pltpu.CompilerParams(
            collective_id=collective_id, has_side_effects=True, vmem_limit_bytes=60000000),
        name="scatter_gradients",
    )(*arrays)


HD = 64
EPS = 1e-05
F32, BF16 = jnp.float32, jnp.bfloat16


def layer_norm(values, gain, shift):
    center = values - jnp.mean(values, axis=-1, keepdims=True)
    inverse = lax.rsqrt(jnp.mean(center * center, axis=-1, keepdims=True) + EPS)
    normed = center * inverse
    return normed * gain.astype(F32) + shift.astype(F32), normed, inverse


def norm_back(grad_out, gain, normed, inverse):
    scaled = grad_out * gain.astype(F32)
    grad_in = inverse * (
        scaled
        - jnp.mean(scaled, axis=-1, keepdims=True)
        - normed * jnp.mean(scaled * normed, axis=-1, keepdims=True)
    )
    return grad_in, jnp.sum(grad_out * normed, axis=0), jnp.sum(grad_out, axis=0)


def dot(left, right, dims=((1,), (0,))):
    return lax.dot_general(left, right, (dims, ((), ())), preferred_element_type=F32)


def rows_of(left, right):
    return dot(left, right, ((0,), (0,)))


def flipped(left, right):
    return dot(left, right, ((1,), (1,)))


def gelu_slope(values):
    cumulative = 0.5 * (1.0 + lax.erf(values * 0.7071067811865476))
    return cumulative + values * jnp.exp(-0.5 * values * values) * 0.3989422804014327


def row_mask(ids):
    length = ids.shape[0]
    places = lax.broadcasted_iota(jnp.int32, (length, length), 0)
    others_ = lax.broadcasted_iota(jnp.int32, (length, length), 1)
    return (ids[:, None] == ids[None, :]) & (ids[None, :] >= 0) | (places == others_)


def row_scores(query, keys, ids):
    scores = jnp.einsum("qhd,khd->hqk", query, keys, preferred_element_type=F32) * HD ** -0.5
    return jnp.where(row_mask(ids)[None], scores, -1e30)


def attend_row(query, keys, values, ids):
    scores = row_scores(query, keys, ids)
    peak = jnp.max(scores, axis=-1, keepdims=True)
    log_total = peak + jnp.log(jnp.sum(jnp.exp(scores - peak), axis=-1, keepdims=True))
    probs = jnp.exp(scores - log_total).astype(BF16)
    return jnp.einsum("hqk,khd->qhd", probs, values, preferred_element_type=F32), log_total


def attend_back(query, keys, values, grad_mixed, ids, log_total):
    probs = jnp.exp(row_scores(query, keys, ids) - log_total)
    grad_values = jnp.einsum("hqk,qhd->khd", probs.astype(BF16), grad_mixed, preferred_element_type=F32)
    grad_probs = jnp.einsum("qhd,khd->hqk", grad_mixed, values, preferred_element_type=F32)
    grad_low = (probs * (grad_probs - jnp.sum(probs * grad_probs, axis=-1, keepdims=True))).astype(BF16)
    scale = HD ** -0.5
    grad_query = jnp.einsum("hqk,khd->qhd", grad_low, keys, preferred_element_type=F32) * scale
    grad_keys = jnp.einsum("hqk,qhd->khd", grad_low, query, preferred_element_type=F32) * scale
    return grad_query.astype(BF16), grad_keys.astype(BF16), grad_values.astype(BF16)


MATRICES = ("wq", "wk", "wv", "wo", "wu", "wd")
COLOURS = (0, 1, 1, 0, 0, 1)
VECTORS = (
    "g1", "s1", "bq", "bv", "g2", "s2", "bo",
    "g3", "s3", "bd", "bu", "g4", "s4",
)
ORDER = (
    "g1", "s1", "wq", "bq", "wk", "wv", "bv",
    "g2", "s2", "wo", "bo", "g3", "s3", "wu",
    "bu", "g4", "s4", "wd", "bd",
)


def pack(vectors):
    flat = jnp.concatenate(vectors, axis=-1)
    size = flat.shape[-1]
    padded = -(-size // 1024) * 1024
    flat = jnp.pad(flat, [(0, 0)] * (flat.ndim - 1) + [(0, padded - size)])
    return flat.reshape(flat.shape[:-1] + (padded // 128, 128))


def fetch(grid, own):
    pieces = [own[name] for name in MATRICES] + [pack([own[name] for name in VECTORS])]
    found = gather_all(grid, pieces, COLOURS + (0,), 0)
    full = {name: got.reshape(-1, got.shape[-1]) for name, got in zip(MATRICES, found)}
    small = found[-1].reshape(-1, pieces[-1].size)
    at = 0
    for name in VECTORS:
        size = own[name].shape[0]
        full[name] = small[:, at : at + size].reshape(-1)
        at += size
    return full


def hand_out(grid, grads, own):
    blocks = grid.blocks()
    count = grid.ny * 2 * grid.nz * grid.nx
    arrays = [grads[name].reshape(blocks + own[name].shape) for name in MATRICES]
    small = pack([grads[name].reshape(count, -1) for name in VECTORS])
    arrays.append(small.reshape(blocks + small.shape[1:]))
    owned = scatter_all(grid, arrays, COLOURS + (0,), 1)
    out = dict(zip(MATRICES, owned))
    small = owned[-1].reshape(-1)
    at = 0
    for name in VECTORS:
        size = own[name].shape[0]
        out[name] = small[at : at + size]
        at += size
    return out


def on_device(grid, inputs, doc_ids, *rest):
    own = dict(zip(ORDER, rest[:-1]))
    cotangent = rest[-1]
    batches, rows, length, width = inputs.shape
    flat = inputs.reshape(-1, width).astype(F32)
    ids = doc_ids.reshape(-1, length)
    p = fetch(grid, own)
    heads = (-1, length, width // HD, HD)

    normed_in, n1, r1 = layer_norm(flat, p["g1"], p["s1"])
    a = normed_in.astype(BF16)
    q = (dot(a, p["wq"]) + p["bq"].astype(F32)).astype(BF16).reshape(heads)
    k = dot(a, p["wk"]).astype(BF16).reshape(heads)
    v = (dot(a, p["wv"]) + p["bv"].astype(F32)).astype(BF16).reshape(heads)
    mixed, totals = [], []
    for i in range(q.shape[0]):
        o, t = attend_row(q[i], k[i], v[i], ids[i])
        mixed.append(o.reshape(length, width))
        totals.append(t)
    o = jnp.concatenate(mixed)
    normed_mid, n2, r2 = layer_norm(o, p["g2"], p["s2"])
    b = normed_mid.astype(BF16)
    x1 = flat + dot(b, p["wo"]) + p["bo"].astype(F32)
    normed_feed, n3, r3 = layer_norm(x1, p["g3"], p["s3"])
    c = normed_feed.astype(BF16)
    u = dot(c, p["wu"]) + p["bu"].astype(F32)
    normed_act, n4, r4 = layer_norm(jax.nn.gelu(u, approximate=False), p["g4"], p["s4"])
    e = normed_act.astype(BF16)
    out = (x1 + dot(e, p["wd"]) + p["bd"].astype(F32)).astype(BF16)

    g = {}
    gd = cotangent.reshape(-1, width)
    gy = gd.astype(F32)
    g["wd"] = rows_of(e, gd).astype(BF16)
    g["bd"] = jnp.sum(gy, axis=0)
    gg, g["g4"], g["s4"] = norm_back(flipped(gd, p["wd"]), p["g4"], n4, r4)
    gu = (gg * gelu_slope(u)).astype(BF16)
    g["wu"] = rows_of(c, gu).astype(BF16)
    g["bu"] = jnp.sum(gu.astype(F32), axis=0)
    gf, g["g3"], g["s3"] = norm_back(flipped(gu, p["wu"]), p["g3"], n3, r3)
    gx1 = gy + gf
    gh = gx1.astype(BF16)
    g["wo"] = rows_of(b, gh).astype(BF16)
    g["bo"] = jnp.sum(gh.astype(F32), axis=0)
    gof, g["g2"], g["s2"] = norm_back(flipped(gh, p["wo"]), p["g2"], n2, r2)
    go = gof.astype(BF16).reshape(heads)
    parts = [attend_back(q[i], k[i], v[i], go[i], ids[i], totals[i]) for i in range(q.shape[0])]
    gq, gk, gv = (jnp.concatenate([part[j].reshape(length, width) for part in parts]) for j in range(3))
    g["wq"] = rows_of(a, gq).astype(BF16)
    g["bq"] = jnp.sum(gq.astype(F32), axis=0)
    g["wk"] = rows_of(a, gk).astype(BF16)
    g["wv"] = rows_of(a, gv).astype(BF16)
    g["bv"] = jnp.sum(gv.astype(F32), axis=0)
    ga = flipped(gq, p["wq"]) + flipped(gk, p["wk"]) + flipped(gv, p["wv"])
    gf1, g["g1"], g["s1"] = norm_back(ga, p["g1"], n1, r1)
    input_grad = (gx1 + gf1).astype(BF16)
    got = hand_out(grid, g, own)
    return (out.reshape(inputs.shape), input_grad.reshape(inputs.shape)) + tuple(got[name] for name in ORDER)


def solution(mesh):
    both = ("dp", "shard")
    grid = Grid(mesh.shape["dp"], mesh.shape["shard"])
    rows = P(None, both, None, None)
    params = tuple(P(both, None) if name in MATRICES else P(both) for name in ORDER)
    return jax.shard_map(
        functools.partial(on_device, grid),
        mesh=mesh,
        in_specs=(rows, P(None, both, None)) + params + (rows,),
        out_specs=(rows, rows) + params,
        check_vma=False,
    )
```

```python
import functools

import jax
import jax.numpy as jnp
from jax import lax
from jax.experimental import pallas as pl
from jax.experimental.pallas import tpu as pltpu
from jax.sharding import PartitionSpec as P


EPS = 1e-05
F32, BF16 = jnp.float32, jnp.bfloat16


def dot(left, right, dims=((1,), (0,))):
    return lax.dot_general(left, right, (dims, ((), ())), preferred_element_type=F32)


def flipped(left, right):
    return dot(left, right, ((1,), (1,)))


def eights(values):
    return jnp.sum(values.reshape(values.shape[0] // 8, 8, values.shape[1]), axis=0)


def mean_of(values):
    return jnp.sum(values, axis=-1, keepdims=True) * (1.0 / values.shape[-1])


def normed_of(values):
    center = values - mean_of(values)
    inverse = lax.rsqrt(mean_of(center * center) + EPS)
    return center * inverse, inverse


def feed_kernel(
    tile, chunk, tiles, x1_ref, gd_ref, wu_ref, wd_ref, g3_ref, s3_ref, bd_ref, bu_ref, g4_ref, s4_ref,
    out_ref, gx1_ref, dwu_ref, dwd_ref, d3_ref, dbu_ref, d4_ref,
    act, slope, scaled, turned, below, turned_c, kept_gd, acc, wide_acc, narrow_acc,
):
    step = pl.program_id(0)
    ff = bu_ref.shape[1]
    chunks = ff // chunk

    @pl.when(step == 0)
    def _():
        wide_acc[...] = jnp.zeros_like(wide_acc)
        narrow_acc[...] = jnp.zeros_like(narrow_acc)

    @pl.when(step < tiles)
    def _():
        rows = pl.ds(pl.multiple_of(step * tile, tile), tile)
        x1 = x1_ref[...]
        gd = gd_ref[...]
        gy = gd.astype(F32)
        kept_gd[rows, :] = gd
        n3, r3 = normed_of(x1)
        c = (n3 * g3_ref[...] + s3_ref[...]).astype(BF16)
        turned_c[:, rows] = c.T

        total = jnp.zeros((tile, 1), F32)
        for j in range(chunks):
            cols = slice(j * chunk, (j + 1) * chunk)
            u = dot(c, wu_ref[:, cols]) + bu_ref[:, cols]
            phi = 0.5 + 0.5 * lax.erf(u * 0.7071067811865476)
            g = u * phi
            act[:, cols] = g
            slope[:, cols] = phi + u * (jnp.exp(u * u * -0.5) * 0.3989422804014327)
            total += jnp.sum(g, axis=-1, keepdims=True)
        mean = total * (1.0 / ff)
        total = jnp.zeros((tile, 1), F32)
        for j in range(chunks):
            d = act[:, j * chunk : (j + 1) * chunk] - mean
            total += jnp.sum(d * d, axis=-1, keepdims=True)
        r4 = lax.rsqrt(total * (1.0 / ff) + EPS)

        sum_t = jnp.zeros((tile, 1), F32)
        sum_tn = jnp.zeros((tile, 1), F32)
        acc[...] = x1 + bd_ref[...]
        for j in range(chunks):
            cols = slice(j * chunk, (j + 1) * chunk)
            gain = g4_ref[:, cols]
            n = (act[:, cols] - mean) * r4
            act[:, cols] = n
            e = (n * gain + s4_ref[:, cols]).astype(BF16)
            turned[cols, rows] = e.T
            acc[...] += dot(e, wd_ref[cols, :])
            ge = flipped(gd, wd_ref[cols, :])
            wide_acc[0:8, cols] += eights(ge * n)
            wide_acc[8:16, cols] += eights(ge)
            t = ge * gain
            scaled[:, cols] = t
            sum_t += jnp.sum(t, axis=-1, keepdims=True)
            sum_tn += jnp.sum(t * n, axis=-1, keepdims=True)
        out_ref[...] = acc[...].astype(BF16)
        mean_t = sum_t * (1.0 / ff)
        mean_tn = sum_tn * (1.0 / ff)
        gc = jnp.zeros_like(x1)
        for j in range(chunks):
            cols = slice(j * chunk, (j + 1) * chunk)
            gg = r4 * (scaled[:, cols] - mean_t - act[:, cols] * mean_tn)
            gu = (gg * slope[:, cols]).astype(BF16)
            below[rows, cols] = gu
            wide_acc[16:24, cols] += eights(gu.astype(F32))
            gc += flipped(gu, wu_ref[:, cols])
        narrow_acc[0:8, :] += eights(gc * n3)
        narrow_acc[8:16, :] += eights(gc)
        narrow_acc[16:24, :] += eights(gy)
        t = gc * g3_ref[...]
        gx1_ref[...] = gy + r3 * (t - mean_of(t) - n3 * mean_of(t * n3))

    @pl.when(step >= tiles)
    def _():
        at = pl.multiple_of((step - tiles) * chunk, chunk)
        dwd_ref[...] = dot(turned[pl.ds(at, chunk), :], kept_gd[...]).astype(BF16)
        dwu_ref[...] = dot(turned_c[...], below[:, pl.ds(at, chunk)]).astype(BF16)

    @pl.when(step == tiles)
    def _():
        d3_ref[...] = jnp.sum(narrow_acc[...].reshape(3, 8, -1), axis=1)
        wide = jnp.sum(wide_acc[...].reshape(3, 8, -1), axis=1)
        d4_ref[...] = wide[0:2]
        dbu_ref[...] = wide[2:3]


def feed(x1, gd, wu, wd, g3, s3, bd, bu, g4, s4, tile=256, chunk=512):
    tokens, width = x1.shape
    ff = wu.shape[1]
    tiles, chunks = tokens // tile, ff // chunk
    row = pl.BlockSpec((tile, width), lambda i: (jnp.minimum(i, tiles - 1), 0))
    whole = lambda a: pl.BlockSpec(a.shape, lambda i: (0, 0), pipeline_mode=pl.Buffered(1))
    late = lambda i: jnp.maximum(i - tiles, 0)
    sds = jax.ShapeDtypeStruct
    return pl.pallas_call(
        functools.partial(feed_kernel, tile, chunk, tiles),
        grid=(tiles + chunks,),
        in_specs=[row, row] + [whole(a) for a in (wu, wd, g3, s3, bd, bu, g4, s4)],
        out_specs=[
            row, row,
            pl.BlockSpec((width, chunk), lambda i: (0, late(i))),
            pl.BlockSpec((chunk, width), lambda i: (late(i), 0)),
            pl.BlockSpec((3, width), lambda i: (0, 0)),
            pl.BlockSpec((1, ff), lambda i: (0, 0)),
            pl.BlockSpec((2, ff), lambda i: (0, 0)),
        ],
        out_shape=[
            sds((tokens, width), BF16), sds((tokens, width), F32), sds((width, ff), BF16), sds((ff, width), BF16),
            sds((3, width), F32), sds((1, ff), F32), sds((2, ff), F32),
        ],
        scratch_shapes=[
            pltpu.VMEM((tile, ff), F32), pltpu.VMEM((tile, ff), F32), pltpu.VMEM((tile, ff), F32),
            pltpu.VMEM((ff, tokens), BF16), pltpu.VMEM((tokens, ff), BF16), pltpu.VMEM((width, tokens), BF16),
            pltpu.VMEM((tokens, width), BF16), pltpu.VMEM((tile, width), F32),
            pltpu.VMEM((24, ff), F32), pltpu.VMEM((24, width), F32),
        ],
        compiler_params=pltpu.CompilerParams(vmem_limit_bytes=64000000),
        name="feed_forward",
    )(x1, gd, wu, wd, g3, s3, bd, bu, g4, s4)


MESH = pl.DeviceIdType.MESH
AXES = ("dp", "shard")


class Grid:
    def __init__(self, dp, shard):
        self.ny = dp // 2
        self.nx = self.ny
        self.nz = shard // self.nx

    def here(self):
        dp, shard = lax.axis_index("dp"), lax.axis_index("shard")
        return dp // 2, dp % 2, shard // self.nx, shard % self.nx

    def device(self, y, c, z, x):
        return (y * 2 + c, z * self.nx + x)

    def blocks(self):
        return (self.ny, 2, self.nz, self.nx)


def others(size, mine):
    return [lax.rem(mine + k, size) for k in range(1, size)]


def greet(grid, y, c, z, x):
    barrier = pltpu.get_barrier_semaphore()
    peers = (
        [(y, c, p, x) for p in others(grid.nz, z)]
        + [(y, c, z, p) for p in others(grid.nx, x)]
        + [(p, c, z, x) for p in others(grid.ny, y)]
        + [(y, 1 - c, z, x)]
    )
    for peer in peers:
        pl.semaphore_signal(barrier, inc=1, device_id=grid.device(*peer), device_id_type=MESH)
    pl.semaphore_wait(barrier, len(peers))


class Gather:
    def __init__(self, grid, place, source, target, colour, send, recv, local):
        self.g, self.place = grid, place
        self.source, self.target, self.colour = source, target, colour
        self.send, self.recv, self.local = send, recv, local

    def plan(self, phase):
        g = self.g
        y, c, z, x = self.place
        t = self.target
        if phase == 0:
            return [(self.source, t.at[y, c, z, x], t.at[y, c, p, x], (y, c, p, x), z, p) for p in others(g.nz, z)]
        if phase == 3:
            return [(t.at[:, c], t.at[:, c], t.at[:, 1 - c], (y, 1 - c, z, x), c, 1 - c)]
        along_x = (phase == 1) == (self.colour == 0)
        if along_x:
            cut = (lambda p: t.at[y, c, :, p]) if phase == 1 else (lambda p: t.at[:, c, :, p])
            return [(cut(x), cut(x), cut(p), (y, c, z, p), x, p) for p in others(g.nx, x)]
        cut = (lambda p: t.at[p, c, :, x]) if phase == 1 else (lambda p: t.at[p, c])
        return [(cut(y), cut(y), cut(p), (p, c, z, x), y, p) for p in others(g.ny, y)]

    def go(self, phase, entry):
        src, dst, _, peer, mine, theirs = entry
        return pltpu.make_async_remote_copy(
            src_ref=src, dst_ref=dst, send_sem=self.send.at[phase, theirs], recv_sem=self.recv.at[phase, mine],
            device_id=self.g.device(*peer), device_id_type=MESH)

    def come(self, phase, entry):
        _, _, landed, peer, _, theirs = entry
        return pltpu.make_async_remote_copy(
            src_ref=landed, dst_ref=landed, send_sem=self.send.at[phase, theirs], recv_sem=self.recv.at[phase, theirs],
            device_id=self.g.device(*peer), device_id_type=MESH)

    def own(self):
        y, c, z, x = self.place
        return pltpu.make_async_copy(self.source, self.target.at[y, c, z, x], self.local)

    def start(self, phase):
        if phase == 0:
            self.own().start()
        for entry in self.plan(phase):
            self.go(phase, entry).start()

    def arrive(self, phase):
        if phase == 0:
            self.own().wait()
        for entry in self.plan(phase):
            self.come(phase, entry).wait_recv()

    def drain(self):
        for phase in range(4):
            for entry in self.plan(phase):
                self.go(phase, entry).wait_send()


def in_turn(groups, step, last):
    for tick in range(len(groups) + last - 1):
        for phase in range(1, last + 1):
            i = tick - (phase - 1)
            if 0 <= i < len(groups):
                step(phase, groups[i])


def group_jobs(jobs, plan):
    count = 1 + max(part[3] for part in plan)
    return [[job for job, part in zip(jobs, plan) if part[3] == g] for g in range(count)]


def gather_jobs(grid, place, plan, sources, targets, send, recv, local):
    jobs = []
    for n, (i, cols, colour, _) in enumerate(plan):
        cut = slice(None) if cols is None else pl.ds(*cols)
        jobs.append(
            Gather(grid, place, sources[i].at[:, cut], Cut(targets[i], cut), colour, send.at[n], recv.at[n], local.at[n])
        )
    return jobs


class Cut:
    def __init__(self, ref, cut):
        self.ref, self.cut = ref, cut

    @property
    def at(self):
        return self

    def __getitem__(self, key):
        key = key if isinstance(key, tuple) else (key,)
        key = key + (slice(None),) * (len(self.ref.shape) - 1 - len(key))
        return self.ref.at[key + (self.cut,)]


def gather_kernel(grid, plan, count, *refs):
    sources, targets, (send, recv, local) = refs[:count], refs[count : 2 * count], refs[2 * count :]
    place = grid.here()
    greet(grid, *place)
    jobs = gather_jobs(grid, place, plan, sources, targets, send, recv, local)
    groups = group_jobs(jobs, plan)
    for job in jobs:
        job.start(0)

    def step(phase, group):
        for job in group:
            job.arrive(phase - 1)
        for job in group:
            job.start(phase)

    in_turn(groups, step, 3)
    for job in jobs:
        job.arrive(3)
    for job in jobs:
        job.drain()


def gather_all(grid, pieces, plan, collective_id):
    n = len(pieces)
    wide = max(grid.nx, grid.ny, grid.nz, 2)
    return pl.pallas_call(
        functools.partial(gather_kernel, grid, plan, n),
        out_shape=[jax.ShapeDtypeStruct(grid.blocks() + p.shape, p.dtype) for p in pieces],
        in_specs=[pl.BlockSpec(memory_space=pltpu.VMEM)] * n,
        out_specs=[pl.BlockSpec(memory_space=pl.ANY)] * n,
        scratch_shapes=[
            pltpu.SemaphoreType.DMA((len(plan), 4, wide)),
            pltpu.SemaphoreType.DMA((len(plan), 4, wide)),
            pltpu.SemaphoreType.DMA((len(plan),)),
        ],
        compiler_params=pltpu.CompilerParams(collective_id=collective_id, has_side_effects=True),
        name="gather_parameters",
    )(*pieces)


class Scatter:
    def __init__(self, grid, place, source, target, held, land, colour, send, recv, local):
        self.g, self.place, self.colour = grid, place, colour
        self.source, self.target, self.held, self.land = source, target, held, land
        self.send, self.recv, self.local = send, recv, local

    def along_y(self, phase):
        return (phase == 1) == (self.colour == 0)

    def plan(self, phase):
        g, held, land = self.g, self.held, self.land
        y, c, z, x = self.place
        if phase == 0:
            return [(self.source.at[:, 1 - c], lambda s: land[0], (y, 1 - c, z, x), c, 1 - c)]
        if phase == 3:
            return [(held.at[y, p, x], lambda s: land[3].at[s], (y, c, p, x), z, p) for p in others(g.nz, z)]
        if self.along_y(phase):
            cut = (lambda p: held.at[p]) if phase == 1 else (lambda p: held.at[p, :, x])
            return [(cut(p), lambda s: land[phase].at[s], (p, c, z, x), y, p) for p in others(g.ny, y)]
        cut = (lambda p: held.at[:, :, p]) if phase == 1 else (lambda p: held.at[y, :, p])
        return [(cut(p), lambda s: land[phase].at[s], (y, c, z, p), x, p) for p in others(g.nx, x)]

    def own(self):
        return pltpu.make_async_copy(self.source.at[:, self.place[1]], self.held, self.local)

    def go(self, phase, entry):
        src, spot, peer, mine, theirs = entry
        return pltpu.make_async_remote_copy(
            src_ref=src, dst_ref=spot(mine), send_sem=self.send.at[phase, theirs], recv_sem=self.recv.at[phase, mine],
            device_id=self.g.device(*peer), device_id_type=MESH)

    def come(self, phase, entry):
        src, spot, peer, mine, theirs = entry
        return pltpu.make_async_remote_copy(
            src_ref=spot(theirs), dst_ref=spot(theirs), send_sem=self.send.at[phase, theirs],
            recv_sem=self.recv.at[phase, theirs], device_id=self.g.device(*peer), device_id_type=MESH)

    def start(self, phase):
        if phase == 0:
            self.own().start()
        for entry in self.plan(phase):
            self.go(phase, entry).start()

    def finish(self, phase):
        g, held, land = self.g, self.held, self.land
        y, c, z, x = self.place
        if phase == 0:
            self.own().wait()
        plan = self.plan(phase)
        for entry in plan:
            self.come(phase, entry).wait_recv()
        kind = held.dtype
        f32 = jnp.float32

        def add(at, parts, out=None):
            total = held[at].astype(f32)
            for part in parts:
                total = total + part.astype(f32)
            if out is None:
                held[at] = total.astype(kind)
            else:
                out[...] = total

        slots = [entry[4] for entry in plan]
        if phase == 0:
            def body(i, carry):
                at = (i // (g.nz * g.nx), i // g.nx % g.nz, i % g.nx)
                add(at, [land[0][at]])
                return carry
            lax.fori_loop(0, g.ny * g.nz * g.nx, body, 0)
        elif phase == 3:
            add((y, z, x), [land[3][s] for s in slots], self.target)
        elif phase == 1 and self.along_y(1):
            def body(i, carry):
                add((y, i // g.nx, i % g.nx), [land[1][s, i // g.nx, i % g.nx] for s in slots])
                return carry
            lax.fori_loop(0, g.nz * g.nx, body, 0)
        elif phase == 1:
            def body(i, carry):
                add((i // g.nz, i % g.nz, x), [land[1][s, i // g.nz, i % g.nz] for s in slots])
                return carry
            lax.fori_loop(0, g.ny * g.nz, body, 0)
        else:
            def body(i, carry):
                add((y, i, x), [land[2][s, i] for s in slots])
                return carry
            lax.fori_loop(0, g.nz, body, 0)

    def drain(self):
        for phase in range(4):
            for entry in self.plan(phase):
                self.go(phase, entry).wait_send()


def scatter_scratch(grid, piece, kind, colour):
    ny, nz, nx = grid.ny, grid.nz, grid.nx
    if colour == 0:
        one, two = (ny, nz, nx), (nx, nz)
    else:
        one, two = (nx, ny, nz), (ny, nz)
    return [pltpu.VMEM(s + piece, kind) for s in ((ny, nz, nx), (ny, nz, nx), one, two, (nz,))]


def scatter_jobs(grid, place, plan, sources, targets, bufs, send, recv, local):
    jobs = []
    for n, (i, cols, colour, _) in enumerate(plan):
        cut = slice(None) if cols is None else pl.ds(*cols)
        jobs.append(
            Scatter(grid, place, Cut(sources[i], cut), targets[i].at[:, cut], bufs[5 * n], bufs[5 * n + 1 : 5 * n + 5],
                    colour, send.at[n], recv.at[n], local.at[n])
        )
    return jobs


def scatter_kernel(grid, plan, count, *refs):
    sources, targets = refs[:count], refs[count : 2 * count]
    bufs = refs[2 * count : 2 * count + 5 * len(plan)]
    send, recv, local = refs[2 * count + 5 * len(plan) :]
    place = grid.here()
    greet(grid, *place)
    jobs = scatter_jobs(grid, place, plan, sources, targets, bufs, send, recv, local)
    groups = group_jobs(jobs, plan)
    for job in jobs:
        job.start(0)

    def step(phase, group):
        for job in group:
            job.finish(phase - 1)
            job.start(phase)

    in_turn(groups, step, 3)
    for job in jobs:
        job.finish(3)
    for job in jobs:
        job.drain()


def scatter_buffers(grid, arrays, plan):
    scratch = []
    for i, cols, colour, _ in plan:
        a = arrays[i]
        scratch += scatter_scratch(grid, (a.shape[4], a.shape[5] if cols is None else cols[1]), a.dtype, colour)
    return scratch


def scatter_all(grid, arrays, plan, collective_id):
    n = len(arrays)
    wide = max(grid.nx, grid.ny, grid.nz, 2)
    return pl.pallas_call(
        functools.partial(scatter_kernel, grid, plan, n),
        out_shape=[jax.ShapeDtypeStruct(a.shape[4:], F32) for a in arrays],
        in_specs=[pl.BlockSpec(memory_space=pl.ANY)] * n,
        out_specs=[pl.BlockSpec(memory_space=pltpu.VMEM)] * n,
        scratch_shapes=scatter_buffers(grid, arrays, plan) + [
            pltpu.SemaphoreType.DMA((len(plan), 4, wide)),
            pltpu.SemaphoreType.DMA((len(plan), 4, wide)),
            pltpu.SemaphoreType.DMA((len(plan),)),
        ],
        compiler_params=pltpu.CompilerParams(
            collective_id=collective_id, has_side_effects=True, vmem_limit_bytes=60000000),
        name="scatter_gradients",
    )(*arrays)


PAIR = 128
HALF = 64


def halves():
    lane = lax.broadcasted_iota(jnp.int32, (1, PAIR), 1)
    low = jnp.where(lane < HALF, 1.0, 0.0)
    return low.astype(BF16), (1.0 - low).astype(BF16)


def stack_heads(values):
    low, high = halves()
    return jnp.concatenate([values * low, values * high], axis=0)


def merge_heads(values):
    half = values.shape[0] // 2
    lane = lax.broadcasted_iota(jnp.int32, (half, PAIR), 1)
    return jnp.where(lane < HALF, values[:half], values[half:])


def bias_of(ids):
    length = ids.shape[1]
    across = jnp.broadcast_to(ids.astype(F32), (PAIR, length))
    down = across.T[:, 0:1]
    across = jnp.broadcast_to(across[0:1], (length, length))
    key = lax.broadcasted_iota(jnp.int32, (length, length), 0)
    query = lax.broadcasted_iota(jnp.int32, (length, length), 1)
    met = ((down == across) & (down >= 0.0)) | (key == query)
    return jnp.where(met, 0.0, -1e30)


def mixer_forward_kernel(
    length, x_ref, ids_ref, wq_ref, wk_ref, wv_ref, wo_ref, g1_ref, s1_ref, bq_ref, bv_ref, g2_ref, s2_ref, bo_ref,
    q_ref, k_ref, v_ref, o_ref, total_ref, x1_ref, bias,
):
    step = pl.program_id(0)
    width = x_ref.shape[1]
    pairs = width // PAIR
    part = lax.rem(step, pairs + 2)

    @pl.when(part == 0)
    def _():
        bias[...] = bias_of(ids_ref[0])
        n1, _ = normed_of(x_ref[...].astype(F32))
        a = (n1 * g1_ref[...] + s1_ref[...]).astype(BF16)
        q = ((dot(a, wq_ref[...]) + bq_ref[...]).astype(BF16) * 0.125).astype(BF16)
        k = dot(a, wk_ref[...]).astype(BF16)
        v = (dot(a, wv_ref[...]) + bv_ref[...]).astype(BF16)
        for h in range(pairs):
            cols = slice(h * PAIR, (h + 1) * PAIR)
            q_ref[h], k_ref[h], v_ref[h] = q[:, cols], k[:, cols], v[:, cols]

    @pl.when((part > 0) & (part <= pairs))
    def _():
        h = jnp.clip(part - 1, 0, pairs - 1)
        scores = flipped(stack_heads(k_ref[h]), q_ref[h])
        turned = v_ref[h].T
        mixed = []
        for i in range(2):
            s = scores[i * length : (i + 1) * length] + bias[...]
            peak = jnp.max(s, axis=0, keepdims=True)
            e = jnp.exp(s - peak)
            total = jnp.sum(e, axis=0, keepdims=True)
            total_ref[0, h, i : i + 1, :] = peak + jnp.log(total)
            mixed.append(dot(turned[i * HALF : (i + 1) * HALF], e.astype(BF16)) * (1.0 / total))
        o_ref[h] = jnp.concatenate(mixed, axis=0).T

    @pl.when(part == pairs + 1)
    def _():
        o = jnp.concatenate([o_ref[h] for h in range(pairs)], axis=1)
        n2, _ = normed_of(o)
        b = (n2 * g2_ref[...] + s2_ref[...]).astype(BF16)
        x1_ref[...] = x_ref[...].astype(F32) + dot(b, wo_ref[...]) + bo_ref[...]


def mixer_forward(x, ids, wq, wk, wv, wo, g1, s1, bq, bv, g2, s2, bo):
    rows, _, length = ids.shape
    tokens, width = x.shape
    pairs = width // PAIR
    steps = pairs + 2
    sds = jax.ShapeDtypeStruct
    whole = lambda a: pl.BlockSpec(a.shape, lambda i: (0, 0), pipeline_mode=pl.Buffered(1))
    flat = pl.BlockSpec((length, width), lambda i: (i // steps, 0))
    heads = pl.BlockSpec((pairs, length, PAIR), lambda i: (0, i // steps, 0))
    split = lambda kind: sds((pairs, tokens, PAIR), kind)
    return pl.pallas_call(
        functools.partial(mixer_forward_kernel, length),
        grid=(rows * steps,),
        in_specs=[flat, pl.BlockSpec((1, 1, length), lambda i: (i // steps, 0, 0))]
        + [whole(a) for a in (wq, wk, wv, wo, g1, s1, bq, bv, g2, s2, bo)],
        out_specs=[heads] * 4 + [pl.BlockSpec((1, pairs, 2, length), lambda i: (i // steps, 0, 0, 0)), flat],
        out_shape=[split(BF16)] * 3 + [split(F32), sds((rows, pairs, 2, length), F32), sds((tokens, width), F32)],
        scratch_shapes=[pltpu.VMEM((length, length), F32)],
        compiler_params=pltpu.CompilerParams(vmem_limit_bytes=64000000),
        name="mixer_forward",
    )(x, ids, wq, wk, wv, wo, g1, s1, bq, bv, g2, s2, bo)


def mixer_backward_kernel(
    length, gx1_ref, x_ref, o_ref, q_ref, k_ref, v_ref, total_ref, ids_ref, wq_ref, wk_ref, wv_ref, wo_ref,
    g1_ref, s1_ref, g2_ref, s2_ref,
    gx_ref, dwq_ref, dwk_ref, dwv_ref, dwo_ref, small_ref,
    go, gh, grads, turned_a, turned_b, delta, bias, sums,
):
    step = pl.program_id(0)
    tokens, width = x_ref.shape
    pairs = width // PAIR
    rows = tokens // length
    work = rows * pairs

    @pl.when(step == 0)
    def _():
        sums[...] = jnp.zeros_like(sums)

    @pl.when(step < rows)
    def _():
        at = pl.ds(pl.multiple_of(step * length, length), length)
        gx1 = gx1_ref[at, :]
        low = gx1.astype(BF16)
        gh[at, :] = low
        gb = flipped(low, wo_ref[...])
        o = jnp.concatenate([o_ref[h, at, :] for h in range(pairs)], axis=1)
        n2, r2 = normed_of(o)
        turned_b[:, at] = (n2 * g2_ref[...] + s2_ref[...]).astype(BF16).T
        sums[0:8, :] += eights(gb * n2)
        sums[8:16, :] += eights(gb)
        sums[16:24, :] += eights(low.astype(F32))
        t = gb * g2_ref[...]
        low = (r2 * (t - mean_of(t) - n2 * mean_of(t * n2))).astype(BF16)
        product = low.astype(F32) * o
        for h in range(pairs):
            cols = slice(h * PAIR, (h + 1) * PAIR)
            go[h, at, :] = low[:, cols]
            turned = product[:, cols].T
            delta[h, 0:1, at] = jnp.sum(turned[:HALF], axis=0, keepdims=True)
            delta[h, 1:2, at] = jnp.sum(turned[HALF:], axis=0, keepdims=True)
        n1, _ = normed_of(x_ref[at, :].astype(F32))
        turned_a[:, at] = (n1 * g1_ref[...] + s1_ref[...]).astype(BF16).T

    @pl.when(step == rows)
    def _():
        dwo_ref[...] = dot(turned_b[...], gh[...]).astype(BF16)

    first = rows + 1

    @pl.when((step >= first) & (step < first + work))
    def _():
        i = jnp.clip(step - first, 0, work - 1)
        r, h = i // pairs, lax.rem(i, pairs)
        at = pl.ds(pl.multiple_of(r * length, length), length)

        @pl.when(h == 0)
        def _():
            bias[...] = bias_of(ids_ref[r])

        q, k, v, g = q_ref[h, at, :], k_ref[h, at, :], v_ref[h, at, :], go[h, at, :]
        scores = flipped(stack_heads(k), q)
        back = flipped(stack_heads(v), g)
        turned = k.T
        soft, sharp, found = [], [], []
        for j in range(2):
            cut = slice(j * length, (j + 1) * length)
            p = jnp.exp(scores[cut] + bias[...] - total_ref[r, h, j : j + 1, :])
            ds = (p * (back[cut] - delta[h, j : j + 1, at])).astype(BF16)
            soft.append(p.astype(BF16))
            sharp.append(ds)
            found.append(dot(turned[j * HALF : (j + 1) * HALF], ds))
        grads[2, h, at, :] = merge_heads(dot(jnp.concatenate(soft, axis=0), g)).astype(BF16)
        grads[1, h, at, :] = merge_heads(dot(jnp.concatenate(sharp, axis=0), q)).astype(BF16)
        grads[0, h, at, :] = (jnp.concatenate(found, axis=0).T * 0.125).astype(BF16)

    second = first + work

    def joined(which, at):
        return jnp.concatenate([grads[which, h, at, :] for h in range(pairs)], axis=1)

    @pl.when(step == second)
    def _():
        every = slice(None)
        dwq_ref[...] = dot(turned_a[...], joined(0, every)).astype(BF16)
        dwk_ref[...] = dot(turned_a[...], joined(1, every)).astype(BF16)
        dwv_ref[...] = dot(turned_a[...], joined(2, every)).astype(BF16)

    @pl.when(step > second)
    def _():
        r = jnp.clip(step - second - 1, 0, rows - 1)
        at = pl.ds(pl.multiple_of(r * length, length), length)
        gq, gk, gv = joined(0, at), joined(1, at), joined(2, at)
        ga = flipped(gq, wq_ref[...]) + flipped(gk, wk_ref[...]) + flipped(gv, wv_ref[...])
        n1, r1 = normed_of(x_ref[at, :].astype(F32))
        sums[24:32, :] += eights(ga * n1)
        sums[32:40, :] += eights(ga)
        sums[40:48, :] += eights(gq.astype(F32))
        sums[48:56, :] += eights(gv.astype(F32))
        t = ga * g1_ref[...]
        gx_ref[at, :] = (gx1_ref[at, :] + r1 * (t - mean_of(t) - n1 * mean_of(t * n1))).astype(BF16)
        small_ref[...] = jnp.sum(sums[...].reshape(7, 8, width), axis=1)


def mixer_backward(gx1, x, o, q, k, v, total, ids, wq, wk, wv, wo, g1, s1, g2, s2):
    rows, _, length = ids.shape
    tokens, width = x.shape
    pairs = width // PAIR
    sds = jax.ShapeDtypeStruct
    vmem = pl.BlockSpec(memory_space=pltpu.VMEM)
    return pl.pallas_call(
        functools.partial(mixer_backward_kernel, length),
        grid=(rows + 1 + rows * pairs + 1 + rows,),
        in_specs=[vmem] * 16,
        out_specs=[vmem] * 6,
        out_shape=[sds((tokens, width), BF16)] + [sds((width, width), BF16)] * 4 + [sds((7, width), F32)],
        scratch_shapes=[
            pltpu.VMEM((pairs, tokens, PAIR), BF16), pltpu.VMEM((tokens, width), BF16),
            pltpu.VMEM((3, pairs, tokens, PAIR), BF16), pltpu.VMEM((width, tokens), BF16),
            pltpu.VMEM((width, tokens), BF16), pltpu.VMEM((pairs, 2, tokens), F32),
            pltpu.VMEM((length, length), F32), pltpu.VMEM((56, width), F32),
        ],
        compiler_params=pltpu.CompilerParams(vmem_limit_bytes=64000000),
        name="mixer_backward",
    )(gx1, x, o, q, k, v, total, ids, wq, wk, wv, wo, g1, s1, g2, s2)


MATRICES = ("wq", "wk", "wv", "wo", "wu", "wd")
VECTORS = ("g1", "s1", "bq", "bv", "g2", "s2", "bo", "g3", "s3", "bd", "bu", "g4", "s4")
ORDER = (
    "g1", "s1", "wq", "bq", "wk", "wv", "bv", "g2", "s2", "wo", "bo", "g3", "s3", "wu", "bu", "g4", "s4", "wd", "bd",
)


def pack(vectors):
    size = sum(v.shape[-1] for v in vectors)
    padded = -(-size // 1024) * 1024
    flat, at = 0, 0
    for v in vectors:
        flat = flat + jnp.pad(v, [(0, 0)] * (v.ndim - 1) + [(at, padded - at - v.shape[-1])])
        at += v.shape[-1]
    return flat.reshape(flat.shape[:-1] + (padded // 128, 128))


def halved(i, cols, pieces, colour, group):
    size = cols // pieces
    return [(i, (n * size, size), (colour + n) % 2, group + n) for n in range(pieces)]


def fetch(grid, own):
    pieces = [own[name] for name in MATRICES] + [pack([own[name] for name in VECTORS])]
    plan = [(6, None, 0, 0), (0, None, 0, 0), (1, None, 1, 0), (2, None, 0, 1), (3, None, 1, 1)]
    plan += halved(4, own["wu"].shape[1], 6, 0, 2) + halved(5, own["wd"].shape[1], 6, 1, 2)
    found = gather_all(grid, pieces, plan, 0)
    full = {name: got.reshape(-1, got.shape[-1]) for name, got in zip(MATRICES, found)}
    small = found[-1].reshape(-1, pieces[-1].size)
    at = 0
    for name in VECTORS:
        size = own[name].shape[0]
        full[name] = small[:, at : at + size].reshape(1, -1).astype(F32)
        at += size
    return full


def hand_out(grid, grads, own):
    blocks = grid.blocks()
    count = grid.ny * 2 * grid.nz * grid.nx
    arrays = [grads[name].reshape(blocks + own[name].shape) for name in MATRICES]
    small = pack([grads[name].reshape(count, -1) for name in VECTORS])
    arrays.append(small.reshape(blocks + small.shape[1:]))
    plan = halved(4, own["wu"].shape[1], 6, 0, 0) + halved(5, own["wd"].shape[1], 6, 1, 0)
    plan += [(6, None, 0, 6), (0, None, 0, 6), (1, None, 1, 6), (2, None, 0, 7), (3, None, 1, 7)]
    owned = scatter_all(grid, arrays, plan, 1)
    out = dict(zip(MATRICES, owned))
    small = owned[-1].reshape(-1)
    at = 0
    for name in VECTORS:
        size = own[name].shape[0]
        out[name] = small[at : at + size]
        at += size
    return out


def on_device(grid, inputs, doc_ids, *rest):
    own = dict(zip(ORDER, rest[:-1]))
    width = inputs.shape[-1]
    x = inputs.reshape(-1, width)
    ids = doc_ids.reshape(-1, 1, doc_ids.shape[-1])
    gd = rest[-1].reshape(-1, width)
    p = fetch(grid, own)
    q, k, v, o, total, x1 = mixer_forward(
        x, ids, *(p[n] for n in ("wq", "wk", "wv", "wo", "g1", "s1", "bq", "bv", "g2", "s2", "bo"))
    )
    g = {}
    out, gx1, g["wu"], g["wd"], d3, g["bu"], d4 = feed(
        x1, gd, *(p[n] for n in ("wu", "wd", "g3", "s3", "bd", "bu", "g4", "s4"))
    )
    input_grad, g["wq"], g["wk"], g["wv"], g["wo"], small = mixer_backward(
        gx1, x, o, q, k, v, total, ids, *(p[n] for n in ("wq", "wk", "wv", "wo", "g1", "s1", "g2", "s2"))
    )
    g["g3"], g["s3"], g["bd"] = d3
    g["g4"], g["s4"] = d4
    g["g2"], g["s2"], g["bo"], g["g1"], g["s1"], g["bq"], g["bv"] = small
    got = hand_out(grid, g, own)
    return (out.reshape(inputs.shape), input_grad.reshape(inputs.shape)) + tuple(got[name] for name in ORDER)


def solution(mesh):
    both = ("dp", "shard")
    grid = Grid(mesh.shape["dp"], mesh.shape["shard"])
    rows = P(None, both, None, None)
    params = tuple(P(both, None) if name in MATRICES else P(both) for name in ORDER)
    return jax.shard_map(
        functools.partial(on_device, grid),
        mesh=mesh,
        in_specs=(rows, P(None, both, None)) + params + (rows,),
        out_specs=(rows, rows) + params,
        check_vma=False,
    )
```
